32 devices in a mesh: prow: 8 (over z, core), pcol: 4 (over y, x).
Axes of the slice: x: 2, y: 2, z: 4, core: 2. Of those that a mesh axis runs over, the one named last changes fastest.
Arguments:
- right_side: float32 [1024, 4, 4, 1024], P('prow', None, 'pcol'), may hold values from -6 to 6
- inverse_blocks: bfloat16 [2, 1, 8, 1024, 2, 4, 1024], P(None, None, 'prow', None, None, 'pcol'), as said below
- coupling: bfloat16 [1, 8, 1024, 2, 4, 1024], P(None, 'prow', None, None, 'pcol'), may hold values from -0.03125 to 0.03125
- pivots: int32 [2, 8, 1024], P(None, 'prow'), may hold values from 0 to 16383, as said below
Outputs:
- solution: bfloat16 [1024, 2, 8, 1024], P('pcol', None, 'prow')
The draws below stay inside these ranges and needn't reach their ends.
Inputs may be any that keep to these rules, and one draw needn't show every extreme that they name: `inverse_blocks`: each block is unit upper triangular: ones on its diagonal, zeros below it. Every row number of the window appears exactly once; for every p and p2, exactly 16 * 1024 / 8 ** 2 of the entries pivots[:, p, :] are rows g with (g // 1024) % 8 == p2.
All inputs are finite; a program needn't handle non-finite values.
Results may differ from the reference program's by a relative error of at most 0.0052.
Values may be sent and summed in bfloat16 or wider, within the bound.
A program may use at most 128 MiB of HBM per device.

```python
import math
import jax
import jax.numpy as jnp
from jax import lax

NB = 1024
NRHS = 1024
SB = 8
WT = 16
N_PROW = 8
N_PCOL = 4


def draw_inverse_blocks(key, part):
    block_span = SB * NB
    row_ids = lax.broadcasted_iota(jnp.int32, (block_span, block_span), 0)
    col_ids = lax.broadcasted_iota(jnp.int32, (block_span, block_span), 1)
    upper_mask = (col_ids > row_ids).astype(jnp.float32)
    diagonal = (col_ids == row_ids).astype(jnp.float32)
    keys = jax.random.split(key, 4)

    def one_block(noise_key, scale_key):
        noise = jax.random.normal(noise_key, (block_span, block_span), jnp.float32)
        return diagonal + upper_mask * noise * (0.7 / math.sqrt(block_span))
    blocks = jnp.stack([one_block(keys[0], keys[1]), one_block(keys[2], keys[3])])
    return blocks.reshape(2, SB // N_PROW, N_PROW, NB, SB // N_PCOL, N_PCOL, NB).astype(jnp.bfloat16)


def draw_pivots(key, part):
    local_rows = WT // N_PROW * NB
    share = local_rows // N_PROW
    source_keys = jax.random.split(jax.random.fold_in(key, 11), N_PROW)
    target_keys = jax.random.split(jax.random.fold_in(key, 23), N_PROW)
    source_local = jax.vmap(lambda k: jax.random.permutation(k, local_rows))(source_keys).astype(jnp.int32)
    source_ids = lax.broadcasted_iota(jnp.int32, (N_PROW, local_rows), 0)
    global_rows = (source_local // NB * N_PROW + source_ids) * NB + source_local % NB
    grouped = global_rows.reshape(N_PROW, N_PROW, share).transpose(1, 0, 2).reshape(N_PROW, local_rows)
    shuffle = jax.vmap(lambda k: jax.random.permutation(k, local_rows))(target_keys).astype(jnp.int32)
    target_lists = jnp.take_along_axis(grouped, shuffle, axis=1)
    return target_lists.reshape(N_PROW, WT // N_PROW, NB).transpose(1, 0, 2).astype(jnp.int32)


def steps_of(own_key, shape, shards, smallest, largest):
    level, own = 1.0, jax.random.fold_in(own_key, 6)
    for dim, parts in shards:
        draws = jnp.exp(jax.random.uniform(jax.random.fold_in(own, dim), (parts,), jnp.float32, smallest / len(shards), largest / len(shards)))
        level = level * jnp.repeat(draws, shape[dim] // parts).reshape([-1 if axis == dim else 1 for axis in range(len(shape))])
    return level


def bell_draw(rng, shape, deviation, limit, cuts=(), kind=jnp.bfloat16):
    result = jax.random.normal(rng, shape, jnp.float32) * deviation
    if len(cuts) > 0:
        result = steps_of(rng, shape, cuts, -0.22, 0.18) * result
    return jnp.clip(result, min=-limit, max=limit).astype(kind)


def setup_inputs(seed: int = 0) -> dict:
    key_of = jax.random.split(jax.random.key(seed), 5)
    return {
        "right_side": bell_draw(key_of[0], (NRHS, WT // N_PCOL, N_PCOL, NB), 1.0, 6.0, ((0, 8), (2, 4)), jnp.float32),
        "inverse_blocks": draw_inverse_blocks(jax.random.fold_in(key_of[4], 71), 0),
        "coupling": bell_draw(key_of[2], (SB // N_PROW, N_PROW, NB, SB // N_PCOL, N_PCOL, NB), (4 * SB * NB) ** -0.5, 0.03125, ((1, 8), (4, 4))),
        "pivots": draw_pivots(jax.random.fold_in(key_of[4], 71), 0),
    }


def reference(right_side, inverse_blocks, coupling, pivots):
    block_span = SB * NB
    window_rhs = right_side.reshape(NRHS, WT * NB)
    inverse_pair = inverse_blocks.reshape(2, block_span, block_span)
    coupling_mat = coupling.reshape(block_span, block_span)
    contract_last = (((1,), (1,)), ((), ()))
    upper_ready = window_rhs[:, block_span:].astype(jnp.bfloat16)
    upper_solved = lax.dot_general(upper_ready, inverse_pair[1], contract_last, preferred_element_type=jnp.float32).astype(jnp.bfloat16)
    update = jnp.dot(upper_solved, coupling_mat, preferred_element_type=jnp.float32)
    lower_ready = (window_rhs[:, :block_span] - update).astype(jnp.bfloat16)
    lower_solved = lax.dot_general(lower_ready, inverse_pair[0], contract_last, preferred_element_type=jnp.float32).astype(jnp.bfloat16)
    joined = jnp.concatenate([lower_solved, upper_solved], axis=1)
    permuted = jnp.take(joined, pivots.reshape(WT * NB).astype(jnp.int32), axis=1)
    return permuted.reshape(NRHS, WT // N_PROW, N_PROW, NB)
```

```python
import jax
import jax.numpy as jnp
from jax import lax
from jax.sharding import PartitionSpec as P


def body(right_side, inverse_blocks, coupling, pivots):
    bf16 = jnp.bfloat16
    f32 = jnp.float32
    rhs_here = right_side.shape[0]
    tiles_across = right_side.shape[1]
    tile_width = right_side.shape[3]
    blocks_here = inverse_blocks.shape[1]
    count_rows = blocks_here * tile_width
    tiles_half = inverse_blocks.shape[4]
    count_cols = tiles_half * tile_width
    inverse_pair = inverse_blocks.reshape(2, count_rows, count_cols)
    coupling_mat = coupling.reshape(count_rows, count_cols)
    rows_axis = lax.axis_size("prow")
    cols_axis = lax.axis_size("pcol")
    own_cols = rhs_here * rows_axis // cols_axis
    contract_last = (((1,), (1,)), ((), ()))
    me = lax.axis_index("prow")

    lower_rhs = right_side[:, :tiles_half].reshape(rhs_here, count_cols)
    upper_rhs = right_side[:, tiles_half:].astype(bf16).reshape(rhs_here, count_cols)

    own_pivots = pivots.reshape(-1)
    width = own_pivots.shape[0]
    share = width // rows_axis
    all_pivots = lax.all_gather(own_pivots, "prow", axis=0)

    def owner_of(rows):
        return rows // tile_width % rows_axis

    def local_of(rows):
        return rows // (tile_width * rows_axis) * tile_width + rows % tile_width

    mine = owner_of(all_pivots) == me
    slot = jnp.where(mine, jnp.cumsum(mine.astype(jnp.int32), axis=1) - 1, -1)
    hits = slot[:, :, None] == lax.broadcasted_iota(jnp.int32, (1, 1, share), 2)
    picked = jnp.sum(jnp.where(hits, local_of(all_pivots)[:, :, None], 0), axis=1)
    owner = owner_of(own_pivots)
    same = owner[None, :] == lax.broadcasted_iota(jnp.int32, (rows_axis, 1), 0)
    rank = jnp.sum(jnp.where(same, jnp.cumsum(same.astype(jnp.int32), axis=1) - 1, 0), axis=0)
    code = owner * share + rank

    def solve_with(inverse_mat, portion):
        return lax.dot_general(portion, inverse_mat, contract_last, preferred_element_type=bf16)

    first_partial = solve_with(
        inverse_pair[1], lax.all_gather(upper_rhs, "prow", axis=0, tiled=True)
    )
    upper_solved = lax.psum_scatter(first_partial, "pcol", scatter_dimension=0, tiled=True)
    update_partial = jnp.dot(
        lax.all_gather(upper_solved, "pcol", axis=0, tiled=True),
        coupling_mat,
        preferred_element_type=bf16,
    )
    update = lax.psum_scatter(update_partial, "prow", scatter_dimension=0, tiled=True)
    lower_ready = (lower_rhs - update.astype(f32)).astype(bf16)
    second_partial = solve_with(
        inverse_pair[0], lax.all_gather(lower_ready, "prow", axis=0, tiled=True)
    )
    lower_solved = lax.psum_scatter(second_partial, "pcol", scatter_dimension=0, tiled=True)
    joined = jnp.concatenate([lower_solved, upper_solved], axis=1)
    choose = (
        picked.reshape(-1)[None, :] == lax.broadcasted_iota(jnp.int32, (width, 1), 0)
    ).astype(bf16)
    chosen = jnp.dot(joined, choose, preferred_element_type=bf16)
    received = lax.all_to_all(
        chosen.reshape(own_cols, rows_axis, share), "prow", split_axis=1, concat_axis=1
    ).reshape(own_cols, width)
    place = (
        code[None, :] == lax.broadcasted_iota(jnp.int32, (width, 1), 0)
    ).astype(bf16)
    permuted = jnp.dot(received, place, preferred_element_type=bf16)
    return permuted.reshape(own_cols, pivots.shape[0], 1, tile_width)


def solution(mesh):
    in_specs = (
        P("prow", None, "pcol", None),
        P(None, None, "prow", None, None, "pcol", None),
        P(None, "prow", None, None, "pcol", None),
        P(None, "prow", None),
    )
    out_specs = P("pcol", None, "prow", None)
    return jax.shard_map(body, mesh=mesh, in_specs=in_specs, out_specs=out_specs, check_vma=False)
```

```python
import functools

import jax
import jax.numpy as jnp
from jax import lax
from jax.experimental import pallas as pl
from jax.experimental.pallas import tpu as pltpu
from jax.sharding import PartitionSpec as P

BF16 = jnp.bfloat16
F32 = jnp.float32
MESH = pl.DeviceIdType.MESH
PARTS = 2
NT = (((1,), (1,)), ((), ()))
NN = (((1,), (0,)), ((), ()))


def tile_of(size):
    return 256 if size % 256 == 0 else 128


def span(index, size):
    return pl.ds(pl.multiple_of(index * size, size), size)


def meet(sizes):
    barrier = pltpu.get_barrier_semaphore()
    count = 0
    for name, size in sizes:
        place = lax.axis_index(name)
        for step in range(1, size):
            peer = lax.rem(place + step, size)
            pl.semaphore_signal(barrier, inc=1, device_id={name: peer}, device_id_type=MESH)
            count += 1
    pl.semaphore_wait(barrier, count)


def spread_order(size):
    half = size // 2
    return sorted(range(1, size), key=lambda step: (step == half, step))


def start_sums(lhs_ref, mat_ref, own_ref, send_ref, recv_ref, send_sem, recv_sem, size):
    place = lax.axis_index("pcol")
    own, width = own_ref.shape
    tile = tile_of(width)
    part = own // PARTS

    def product(target, store):
        rows = span(target, own)

        @pl.loop(0, width // tile)
        def _(step):
            cols = span(step, tile)
            store(
                cols,
                lax.dot_general(
                    lhs_ref[rows, :], mat_ref[cols, :], NT, preferred_element_type=F32
                ),
            )

    def copy_of(piece, step):
        rows = pl.ds(piece * part, part)
        return pltpu.make_async_remote_copy(
            src_ref=send_ref.at[step - 1, rows],
            dst_ref=recv_ref.at[step - 1, rows],
            send_sem=send_sem.at[piece, step - 1],
            recv_sem=recv_sem.at[piece, step - 1],
            device_id={"pcol": lax.rem(place + step, size)},
            device_id_type=MESH,
        )

    copies = {}
    for step in spread_order(size):

        def keep(cols, value, step=step):
            send_ref[step - 1, :, cols] = value.astype(BF16)

        product(lax.rem(place + step, size), keep)
        copies[0, step] = copy_of(0, step)
        copies[0, step].start()
    for piece in range(1, PARTS):
        for step in spread_order(size):
            copies[piece, step] = copy_of(piece, step)
            copies[piece, step].start()

    def hold(cols, value):
        own_ref[:, cols] = value

    product(place, hold)
    return copies


def finish_sum(copies, piece, own_ref, recv_ref, size):
    own = own_ref.shape[0]
    part = own // PARTS
    rows = pl.ds(piece * part, part)
    for step in spread_order(size):
        copies[piece, step].wait_recv()
    total = own_ref[rows, :]
    for step in range(1, size):
        total = total + recv_ref[step - 1, rows, :].astype(F32)
    return total.astype(BF16)


def upper_kernel(
    size, rhs_ref, inv_ref, coup_ref, upd_ref, solved_ref,
    own_ref, send_ref, recv_ref, full_ref, send_sem, recv_sem, gsend_sem, grecv_sem,
):
    meet((("pcol", size),))
    place = lax.axis_index("pcol")
    own, width = solved_ref.shape
    part = own // PARTS
    count = coup_ref.shape[1]
    tile = tile_of(count)
    copies = start_sums(
        rhs_ref, inv_ref, own_ref, send_ref, recv_ref, send_sem, recv_sem, size
    )
    shares = {}
    for piece in range(PARTS):
        rows = pl.ds(piece * part, part)
        solved_ref[rows, :] = finish_sum(copies, piece, own_ref, recv_ref, size)
        for step in spread_order(size):
            shares[piece, step] = pltpu.make_async_remote_copy(
                src_ref=solved_ref.at[rows],
                dst_ref=full_ref.at[step - 1, rows],
                send_sem=gsend_sem.at[piece, step - 1],
                recv_sem=grecv_sem.at[piece, step - 1],
                device_id={"pcol": lax.rem(place + step, size)},
                device_id_type=MESH,
            )
            shares[piece, step].start()

    def couple(target, block):
        rows = span(target, own)

        @pl.loop(0, count // tile)
        def _(step):
            cols = span(step, tile)
            upd_ref[rows, cols] = lax.dot_general(
                block[...], coup_ref[:, cols], NN, preferred_element_type=F32
            ).astype(BF16)

    couple(place, solved_ref)
    for step in spread_order(size):
        for piece in range(PARTS):
            shares[piece, step].wait_recv()
        couple(lax.rem(place - step + size, size), full_ref.at[step - 1])
    for copy in list(copies.values()) + list(shares.values()):
        copy.wait_send()


def lower_kernel(
    size, line, rhs_ref, inv_ref, upper_ref, picked_ref, code_ref, out_ref,
    own_ref, send_ref, recv_ref, pass_ref, take_ref,
    send_sem, recv_sem, xsend_sem, xrecv_sem,
):
    meet((("pcol", size), ("prow", line)))
    place = lax.axis_index("prow")
    own, width = own_ref.shape
    part = own // PARTS
    share = picked_ref.shape[2]
    count = out_ref.shape[1]
    tile = tile_of(count)
    copies = start_sums(
        rhs_ref, inv_ref, own_ref, send_ref, recv_ref, send_sem, recv_sem, size
    )
    row_ids = lax.broadcasted_iota(jnp.int32, (width, share), 0)
    moves = []
    for piece in range(PARTS):
        rows = pl.ds(piece * part, part)
        lower = finish_sum(copies, piece, own_ref, recv_ref, size)
        upper = upper_ref[rows, :]
        for step in list(range(1, line)) + [0]:
            target = lax.rem(place + step, line)
            wanted = picked_ref[target]
            low = jnp.where(row_ids == wanted, 1.0, 0.0).astype(BF16)
            high = jnp.where(row_ids + width == wanted, 1.0, 0.0).astype(BF16)
            chosen = (
                lax.dot_general(lower, low, NN, preferred_element_type=F32)
                + lax.dot_general(upper, high, NN, preferred_element_type=F32)
            ).astype(BF16)
            if step == 0:
                take_ref[0, rows, :] = chosen
                continue
            pass_ref[step - 1, rows, :] = chosen
            move = pltpu.make_async_remote_copy(
                src_ref=pass_ref.at[step - 1, rows],
                dst_ref=take_ref.at[step, rows],
                send_sem=xsend_sem.at[piece, step - 1],
                recv_sem=xrecv_sem.at[piece, step - 1],
                device_id={"prow": target},
                device_id_type=MESH,
            )
            move.start()
            moves.append(move)
    for move in moves:
        move.wait_recv()
    slot_ids = lax.broadcasted_iota(jnp.int32, (share, tile), 0)

    @pl.loop(0, count // tile)
    def _(step):
        cols = span(step, tile)
        code = code_ref[:, cols]
        total = jnp.zeros((own, tile), F32)
        for source in range(line):
            spot = jnp.where(slot_ids + source * share == code, 1.0, 0.0).astype(BF16)
            total = total + lax.dot_general(
                take_ref[source], spot, NN, preferred_element_type=F32
            )
        out_ref[:, cols] = total.astype(BF16)

    for copy in list(copies.values()) + moves:
        copy.wait_send()


def params(number):
    return pltpu.CompilerParams(
        collective_id=number, has_side_effects=True, vmem_limit_bytes=60 * 1024 * 1024
    )


def in_vmem(count):
    return [pl.BlockSpec(memory_space=pltpu.VMEM)] * count


def sum_scratch(size, own, width):
    return [
        pltpu.VMEM((own, width), F32),
        pltpu.VMEM((size - 1, own, width), BF16),
        pltpu.VMEM((size - 1, own, width), BF16),
    ]


def dma(*shape):
    return pltpu.SemaphoreType.DMA(shape)


def body(right_side, inverse_blocks, coupling, pivots):
    rhs_here = right_side.shape[0]
    tile_width = right_side.shape[3]
    blocks_here = inverse_blocks.shape[1]
    count_rows = blocks_here * tile_width
    tiles_half = inverse_blocks.shape[4]
    count_cols = tiles_half * tile_width
    inverse_pair = inverse_blocks.reshape(2, count_rows, count_cols)
    coupling_mat = coupling.reshape(count_rows, count_cols)
    line = lax.axis_size("prow")
    size = lax.axis_size("pcol")
    rhs_total = rhs_here * line
    own = rhs_total // size
    me = lax.axis_index("prow")

    lower_rhs = right_side[:, :tiles_half].reshape(rhs_here, count_cols)
    upper_rhs = right_side[:, tiles_half:].astype(BF16).reshape(rhs_here, count_cols)

    own_pivots = pivots.reshape(-1)
    width = own_pivots.shape[0]
    share = width // line
    all_pivots = lax.all_gather(own_pivots, "prow", axis=0)

    def owner_of(rows):
        return rows // tile_width % line

    def local_of(rows):
        return rows // (tile_width * line) * tile_width + rows % tile_width

    mine = owner_of(all_pivots) == me
    slot = jnp.where(mine, jnp.cumsum(mine.astype(jnp.int32), axis=1) - 1, -1)
    hits = slot[:, :, None] == lax.broadcasted_iota(jnp.int32, (1, 1, share), 2)
    picked = jnp.sum(jnp.where(hits, local_of(all_pivots)[:, :, None], 0), axis=1)
    owner = owner_of(own_pivots)
    same = owner[None, :] == lax.broadcasted_iota(jnp.int32, (line, 1), 0)
    rank = jnp.sum(jnp.where(same, jnp.cumsum(same.astype(jnp.int32), axis=1) - 1, 0), axis=0)
    code = (me - owner + line) % line * share + rank

    gathered = lax.all_gather(upper_rhs, "prow", axis=0, tiled=True)
    update_partial, upper_solved = pl.pallas_call(
        functools.partial(upper_kernel, size),
        out_shape=(
            jax.ShapeDtypeStruct((rhs_total, count_cols), BF16),
            jax.ShapeDtypeStruct((own, count_rows), BF16),
        ),
        in_specs=in_vmem(3),
        out_specs=tuple(in_vmem(2)),
        scratch_shapes=sum_scratch(size, own, count_rows)
        + [pltpu.VMEM((size - 1, own, count_rows), BF16)]
        + [dma(PARTS, size - 1)] * 4,
        compiler_params=params(0),
        name="upper",
    )(gathered, inverse_pair[1], coupling_mat)
    update = lax.psum_scatter(update_partial, "prow", scatter_dimension=0, tiled=True)
    lower_ready = (lower_rhs - update.astype(F32)).astype(BF16)
    gathered = lax.all_gather(lower_ready, "prow", axis=0, tiled=True)
    permuted = pl.pallas_call(
        functools.partial(lower_kernel, size, line),
        out_shape=jax.ShapeDtypeStruct((own, width), BF16),
        in_specs=in_vmem(5),
        out_specs=in_vmem(1)[0],
        scratch_shapes=sum_scratch(size, own, count_rows)
        + [
            pltpu.VMEM((line - 1, own, share), BF16),
            pltpu.VMEM((line, own, share), BF16),
        ]
        + [dma(PARTS, size - 1)] * 2
        + [dma(PARTS, line - 1)] * 2,
        compiler_params=params(1),
        name="lower",
    )(gathered, inverse_pair[0], upper_solved, picked.reshape(line, 1, share), code.reshape(1, width))
    return permuted.reshape(own, pivots.shape[0], 1, tile_width)


def solution(mesh):
    in_specs = (
        P("prow", None, "pcol", None),
        P(None, None, "prow", None, None, "pcol", None),
        P(None, "prow", None, None, "pcol", None),
        P(None, "prow", None),
    )
    out_specs = P("pcol", None, "prow", None)
    return jax.shard_map(body, mesh=mesh, in_specs=in_specs, out_specs=out_specs, check_vma=False)
```

```python
import functools

import jax
import jax.numpy as jnp
from jax import lax
from jax.experimental import pallas as pl
from jax.experimental.pallas import tpu as pltpu
from jax.sharding import PartitionSpec as P

BF16 = jnp.bfloat16
F32 = jnp.float32
MESH = pl.DeviceIdType.MESH
PARTS = 2
CORES = 2
NT = (((1,), (1,)), ((), ()))
NN = (((1,), (0,)), ((), ()))


def tile_of(size):
    return 256 if size % 256 == 0 else 128


def span(index, size):
    return pl.ds(pl.multiple_of(index * size, size), size)


def meet(sizes):
    barrier = pltpu.get_barrier_semaphore()
    count = 0
    for name, size in sizes:
        place = lax.axis_index(name)
        for step in range(1, size):
            peer = lax.rem(place + step, size)
            pl.semaphore_signal(barrier, inc=1, device_id={name: peer}, device_id_type=MESH)
            count += 1
    pl.semaphore_wait(barrier, count)


def spread_order(size):
    half = size // 2
    return sorted(range(1, size), key=lambda step: (step == half, step))


def start_sums(lhs_ref, mat_ref, own_ref, send_ref, recv_ref, send_sem, recv_sem, size):
    place = lax.axis_index("pcol")
    own, width = own_ref.shape
    tile = tile_of(width)
    part = own // PARTS

    def product(target, store):
        rows = span(target, own)

        @pl.loop(0, width // tile)
        def _(step):
            cols = span(step, tile)
            store(
                cols,
                lax.dot_general(
                    lhs_ref[rows, :], mat_ref[cols, :], NT, preferred_element_type=F32
                ),
            )

    def copy_of(piece, step):
        rows = pl.ds(piece * part, part)
        return pltpu.make_async_remote_copy(
            src_ref=send_ref.at[step - 1, rows],
            dst_ref=recv_ref.at[step - 1, rows],
            send_sem=send_sem.at[piece, step - 1],
            recv_sem=recv_sem.at[piece, step - 1],
            device_id={"pcol": lax.rem(place + step, size)},
            device_id_type=MESH,
        )

    copies = {}
    for step in spread_order(size):

        def keep(cols, value, step=step):
            send_ref[step - 1, :, cols] = value.astype(BF16)

        product(lax.rem(place + step, size), keep)
        copies[0, step] = copy_of(0, step)
        copies[0, step].start()
    for piece in range(1, PARTS):
        for step in spread_order(size):
            copies[piece, step] = copy_of(piece, step)
            copies[piece, step].start()

    def hold(cols, value):
        own_ref[:, cols] = value

    product(place, hold)
    return copies


def finish_sum(copies, piece, own_ref, recv_ref, size):
    own = own_ref.shape[0]
    part = own // PARTS
    rows = pl.ds(piece * part, part)
    for step in spread_order(size):
        copies[piece, step].wait_recv()
    total = own_ref[rows, :]
    for step in range(1, size):
        total = total + recv_ref[step - 1, rows, :].astype(F32)
    return total.astype(BF16)


def upper_kernel(
    size, line, rhs_ref, inv_ref, coup_ref, upd_ref, solved_ref,
    all_ref, prod_ref, own_ref, send_ref, recv_ref, full_ref,
    rsend_sem, rrecv_sem, psend_sem, precv_sem, send_sem, recv_sem, gsend_sem, grecv_sem,
):
    chips = line // CORES
    here = lax.axis_index("prow")
    place = lax.axis_index("pcol")
    chip = here // CORES
    core = lax.rem(here, CORES)
    right = lax.rem(chip + 1, chips) * CORES + core
    left = lax.rem(chip + chips - 1, chips) * CORES + core
    partner = chip * CORES + (CORES - 1 - core)
    peers = [lax.rem(place + step, size) for step in range(1, size)]

    barrier = pltpu.get_barrier_semaphore()
    for device in (right, left, partner):
        pl.semaphore_signal(barrier, inc=1, device_id={"prow": device}, device_id_type=MESH)
    for device in peers:
        pl.semaphore_signal(barrier, inc=1, device_id={"pcol": device}, device_id_type=MESH)
    pl.semaphore_wait(barrier, 3 + len(peers))

    rhs_here, depth = rhs_ref.shape
    rows = CORES * rhs_here
    part = rows // size
    width = inv_ref.shape[0]
    count = coup_ref.shape[1]
    tile = tile_of(width)
    wide = tile_of(count)

    def remote(src, dst, sends, recvs, axis, device):
        return pltpu.make_async_remote_copy(
            src_ref=src, dst_ref=dst, send_sem=sends, recv_sem=recvs,
            device_id={axis: device}, device_id_type=MESH,
        )

    ring, pairs, sums, shares = {}, {}, {}, {}

    def chip_of(stage):
        return lax.rem(chip + chips - stage, chips)

    def collect(stage):
        slot = chip_of(stage) * CORES + core
        source = rhs_ref if stage == 0 else all_ref.at[slot]
        if stage > 0:
            ring[stage - 1].wait_recv()
        if stage < chips - 1:
            ring[stage] = remote(
                source, all_ref.at[slot], rsend_sem.at[stage], rrecv_sem.at[stage], "prow", right
            )
            ring[stage].start()
        pairs[stage] = remote(
            source, all_ref.at[slot], psend_sem.at[stage], precv_sem.at[stage], "prow", partner
        )
        pairs[stage].start()
        if stage == 0:
            all_ref[slot] = rhs_ref[...]
        pairs[stage].wait_recv()

    def multiply(stage):
        first = chip_of(stage) * CORES

        @pl.loop(0, width // tile)
        def _(step):
            cols = span(step, tile)
            lhs = all_ref[pl.ds(first, CORES)].reshape(rows, depth)
            value = lax.dot_general(lhs, inv_ref[cols, :], NT, preferred_element_type=F32)
            for owner in range(size):
                piece = value[owner * part : (owner + 1) * part]
                prod_ref[owner, :, cols] = piece
                send_ref[stage, owner, :, cols] = piece.astype(BF16)

        own_ref[stage] = prod_ref[place]
        for index, peer in enumerate(peers):
            sums[stage, index] = remote(
                send_ref.at[stage, peer], recv_ref.at[stage, index],
                send_sem.at[stage, index], recv_sem.at[stage, index], "pcol", peer,
            )
            sums[stage, index].start()

    def settle(stage):
        total = own_ref[stage]
        for index in range(size - 1):
            sums[stage, index].wait_recv()
            total = total + recv_ref[stage, index].astype(F32)
        full_ref[stage, place] = total.astype(BF16)
        for index, peer in enumerate(peers):
            shares[stage, index] = remote(
                full_ref.at[stage, place], full_ref.at[stage, place],
                gsend_sem.at[stage, index], grecv_sem.at[stage, index], "pcol", peer,
            )
            shares[stage, index].start()

    def couple(stage):
        for index in range(size - 1):
            shares[stage, index].wait_recv()
        target = span(chip_of(stage), rows)
        solved_ref[target, :] = full_ref[stage].reshape(rows, width)

        @pl.loop(0, count // wide)
        def _(step):
            cols = span(step, wide)
            upd_ref[target, cols] = lax.dot_general(
                solved_ref[target, :], coup_ref[:, cols], NN, preferred_element_type=F32
            ).astype(BF16)

    for stage in range(chips + 2):
        if stage < chips:
            collect(stage)
            multiply(stage)
        if 1 <= stage <= chips:
            settle(stage - 1)
        if stage >= 2:
            couple(stage - 2)
    for group in (ring, pairs, sums, shares):
        for copy in group.values():
            copy.wait_send()


def lower_kernel(
    size, line, rhs_ref, inv_ref, upper_ref, picked_ref, code_ref, out_ref,
    own_ref, send_ref, recv_ref, pass_ref, take_ref,
    send_sem, recv_sem, xsend_sem, xrecv_sem,
):
    meet((("pcol", size), ("prow", line)))
    place = lax.axis_index("prow")
    own, width = own_ref.shape
    part = own // PARTS
    share = picked_ref.shape[2]
    count = out_ref.shape[1]
    tile = tile_of(count)
    copies = start_sums(
        rhs_ref, inv_ref, own_ref, send_ref, recv_ref, send_sem, recv_sem, size
    )
    row_ids = lax.broadcasted_iota(jnp.int32, (width, share), 0)
    moves = []
    for piece in range(PARTS):
        rows = pl.ds(piece * part, part)
        lower = finish_sum(copies, piece, own_ref, recv_ref, size)
        upper = upper_ref[rows, :]
        for step in list(range(1, line)) + [0]:
            target = lax.rem(place + step, line)
            wanted = picked_ref[target]
            low = jnp.where(row_ids == wanted, 1.0, 0.0).astype(BF16)
            high = jnp.where(row_ids + width == wanted, 1.0, 0.0).astype(BF16)
            chosen = (
                lax.dot_general(lower, low, NN, preferred_element_type=F32)
                + lax.dot_general(upper, high, NN, preferred_element_type=F32)
            ).astype(BF16)
            if step == 0:
                take_ref[0, rows, :] = chosen
                continue
            pass_ref[step - 1, rows, :] = chosen
            move = pltpu.make_async_remote_copy(
                src_ref=pass_ref.at[step - 1, rows],
                dst_ref=take_ref.at[step, rows],
                send_sem=xsend_sem.at[piece, step - 1],
                recv_sem=xrecv_sem.at[piece, step - 1],
                device_id={"prow": target},
                device_id_type=MESH,
            )
            move.start()
            moves.append(move)
    for move in moves:
        move.wait_recv()
    slot_ids = lax.broadcasted_iota(jnp.int32, (share, tile), 0)

    @pl.loop(0, count // tile)
    def _(step):
        cols = span(step, tile)
        code = code_ref[:, cols]
        total = jnp.zeros((own, tile), F32)
        for source in range(line):
            spot = jnp.where(slot_ids + source * share == code, 1.0, 0.0).astype(BF16)
            total = total + lax.dot_general(
                take_ref[source], spot, NN, preferred_element_type=F32
            )
        out_ref[:, cols] = total.astype(BF16)

    for copy in list(copies.values()) + moves:
        copy.wait_send()


def params(number):
    return pltpu.CompilerParams(
        collective_id=number, has_side_effects=True, vmem_limit_bytes=60 * 1024 * 1024
    )


def in_vmem(count):
    return [pl.BlockSpec(memory_space=pltpu.VMEM)] * count


def sum_scratch(size, own, width):
    return [
        pltpu.VMEM((own, width), F32),
        pltpu.VMEM((size - 1, own, width), BF16),
        pltpu.VMEM((size - 1, own, width), BF16),
    ]


def dma(*shape):
    return pltpu.SemaphoreType.DMA(shape)


def body(right_side, inverse_blocks, coupling, pivots):
    rhs_here = right_side.shape[0]
    tile_width = right_side.shape[3]
    blocks_here = inverse_blocks.shape[1]
    count_rows = blocks_here * tile_width
    tiles_half = inverse_blocks.shape[4]
    count_cols = tiles_half * tile_width
    inverse_pair = inverse_blocks.reshape(2, count_rows, count_cols)
    coupling_mat = coupling.reshape(count_rows, count_cols)
    line = lax.axis_size("prow")
    size = lax.axis_size("pcol")
    rhs_total = rhs_here * line
    own = rhs_total // size
    me = lax.axis_index("prow")

    lower_rhs = right_side[:, :tiles_half].reshape(rhs_here, count_cols)
    upper_rhs = right_side[:, tiles_half:].astype(BF16).reshape(rhs_here, count_cols)

    own_pivots = pivots.reshape(-1)
    width = own_pivots.shape[0]
    share = width // line
    all_pivots = lax.all_gather(own_pivots, "prow", axis=0)

    def owner_of(rows):
        return rows // tile_width % line

    def local_of(rows):
        return rows // (tile_width * line) * tile_width + rows % tile_width

    mine = owner_of(all_pivots) == me
    slot = jnp.where(mine, jnp.cumsum(mine.astype(jnp.int32), axis=1) - 1, -1)
    hits = slot[:, :, None] == lax.broadcasted_iota(jnp.int32, (1, 1, share), 2)
    picked = jnp.sum(jnp.where(hits, local_of(all_pivots)[:, :, None], 0), axis=1)
    owner = owner_of(own_pivots)
    same = owner[None, :] == lax.broadcasted_iota(jnp.int32, (line, 1), 0)
    rank = jnp.sum(jnp.where(same, jnp.cumsum(same.astype(jnp.int32), axis=1) - 1, 0), axis=0)
    code = (me - owner + line) % line * share + rank

    chips = line // CORES
    part = CORES * rhs_here // size
    update_partial, upper_all = pl.pallas_call(
        functools.partial(upper_kernel, size, line),
        out_shape=(
            jax.ShapeDtypeStruct((rhs_total, count_cols), BF16),
            jax.ShapeDtypeStruct((rhs_total, count_rows), BF16),
        ),
        in_specs=in_vmem(3),
        out_specs=tuple(in_vmem(2)),
        scratch_shapes=[
            pltpu.VMEM((line, rhs_here, count_cols), BF16),
            pltpu.VMEM((size, part, count_rows), F32),
            pltpu.VMEM((chips, part, count_rows), F32),
            pltpu.VMEM((chips, size, part, count_rows), BF16),
            pltpu.VMEM((chips, size - 1, part, count_rows), BF16),
            pltpu.VMEM((chips, size, part, count_rows), BF16),
        ]
        + [dma(chips - 1)] * 2
        + [dma(chips)] * 2
        + [dma(chips, size - 1)] * 4,
        compiler_params=params(0),
        name="upper",
    )(upper_rhs, inverse_pair[1], coupling_mat)
    upper_solved = lax.dynamic_slice_in_dim(upper_all, lax.axis_index("pcol") * own, own, 0)
    update = lax.psum_scatter(update_partial, "prow", scatter_dimension=0, tiled=True)
    lower_ready = (lower_rhs - update.astype(F32)).astype(BF16)
    gathered = lax.all_gather(lower_ready, "prow", axis=0, tiled=True)
    permuted = pl.pallas_call(
        functools.partial(lower_kernel, size, line),
        out_shape=jax.ShapeDtypeStruct((own, width), BF16),
        in_specs=in_vmem(5),
        out_specs=in_vmem(1)[0],
        scratch_shapes=sum_scratch(size, own, count_rows)
        + [
            pltpu.VMEM((line - 1, own, share), BF16),
            pltpu.VMEM((line, own, share), BF16),
        ]
        + [dma(PARTS, size - 1)] * 2
        + [dma(PARTS, line - 1)] * 2,
        compiler_params=params(1),
        name="lower",
    )(gathered, inverse_pair[0], upper_solved, picked.reshape(line, 1, share), code.reshape(1, width))
    return permuted.reshape(own, pivots.shape[0], 1, tile_width)


def solution(mesh):
    in_specs = (
        P("prow", None, "pcol", None),
        P(None, None, "prow", None, None, "pcol", None),
        P(None, "prow", None, None, "pcol", None),
        P(None, "prow", None),
    )
    out_specs = P("pcol", None, "prow", None)
    return jax.shard_map(body, mesh=mesh, in_specs=in_specs, out_specs=out_specs, check_vma=False)
```

```python
import functools

import jax
import jax.numpy as jnp
from jax import lax
from jax.experimental import pallas as pl
from jax.experimental.pallas import tpu as pltpu
from jax.sharding import PartitionSpec as P

BF16 = jnp.bfloat16
F32 = jnp.float32
MESH = pl.DeviceIdType.MESH
PARTS = 2
CORES = 2
NT = (((1,), (1,)), ((), ()))
NN = (((1,), (0,)), ((), ()))


def tile_of(size):
    return 256 if size % 256 == 0 else 128


def span(index, size):
    return pl.ds(pl.multiple_of(index * size, size), size)


def meet(sizes):
    barrier = pltpu.get_barrier_semaphore()
    count = 0
    for name, size in sizes:
        place = lax.axis_index(name)
        for step in range(1, size):
            peer = lax.rem(place + step, size)
            pl.semaphore_signal(barrier, inc=1, device_id={name: peer}, device_id_type=MESH)
            count += 1
    pl.semaphore_wait(barrier, count)


def spread_order(size):
    half = size // 2
    return sorted(range(1, size), key=lambda step: (step == half, step))


def start_sums(lhs_ref, mat_ref, own_ref, send_ref, recv_ref, send_sem, recv_sem, size):
    place = lax.axis_index("pcol")
    own, width = own_ref.shape
    tile = tile_of(width)
    part = own // PARTS
    each = own // lhs_ref.shape[1]

    def product(target, store):
        sources = pl.ds(target * each, each)

        @pl.loop(0, width // tile)
        def _(step):
            cols = span(step, tile)
            store(
                cols,
                lax.dot_general(
                    lhs_ref[sources].reshape(own, lhs_ref.shape[2]),
                    mat_ref[cols, :],
                    NT,
                    preferred_element_type=F32,
                ),
            )

    def copy_of(piece, step):
        rows = pl.ds(piece * part, part)
        return pltpu.make_async_remote_copy(
            src_ref=send_ref.at[step - 1, rows],
            dst_ref=recv_ref.at[step - 1, rows],
            send_sem=send_sem.at[piece, step - 1],
            recv_sem=recv_sem.at[piece, step - 1],
            device_id={"pcol": lax.rem(place + step, size)},
            device_id_type=MESH,
        )

    copies = {}
    for step in spread_order(size):

        def keep(cols, value, step=step):
            send_ref[step - 1, :, cols] = value.astype(BF16)

        product(lax.rem(place + step, size), keep)
        copies[0, step] = copy_of(0, step)
        copies[0, step].start()
    for piece in range(1, PARTS):
        for step in spread_order(size):
            copies[piece, step] = copy_of(piece, step)
            copies[piece, step].start()

    def hold(cols, value):
        own_ref[:, cols] = value

    product(place, hold)
    return copies


def finish_sum(copies, piece, own_ref, recv_ref, size):
    own = own_ref.shape[0]
    part = own // PARTS
    rows = pl.ds(piece * part, part)
    for step in spread_order(size):
        copies[piece, step].wait_recv()
    total = own_ref[rows, :]
    for step in range(1, size):
        total = total + recv_ref[step - 1, rows, :].astype(F32)
    return total.astype(BF16)


def upper_kernel(
    size, line, rhs_ref, inv_ref, coup_ref, upd_ref, solved_ref,
    all_ref, prod_ref, own_ref, send_ref, recv_ref, full_ref,
    rsend_sem, rrecv_sem, psend_sem, precv_sem, send_sem, recv_sem, gsend_sem, grecv_sem,
):
    chips = line // CORES
    here = lax.axis_index("prow")
    place = lax.axis_index("pcol")
    chip = here // CORES
    core = lax.rem(here, CORES)
    right = lax.rem(chip + 1, chips) * CORES + core
    left = lax.rem(chip + chips - 1, chips) * CORES + core
    partner = chip * CORES + (CORES - 1 - core)
    peers = [lax.rem(place + step, size) for step in range(1, size)]

    barrier = pltpu.get_barrier_semaphore()
    for device in (right, left, partner):
        pl.semaphore_signal(barrier, inc=1, device_id={"prow": device}, device_id_type=MESH)
    for device in peers:
        pl.semaphore_signal(barrier, inc=1, device_id={"pcol": device}, device_id_type=MESH)
    pl.semaphore_wait(barrier, 3 + len(peers))

    rhs_here, depth = rhs_ref.shape
    rows = CORES * rhs_here
    part = rows // size
    width = inv_ref.shape[0]
    count = coup_ref.shape[1]
    tile = tile_of(width)
    wide = tile_of(count)

    def remote(src, dst, sends, recvs, axis, device):
        return pltpu.make_async_remote_copy(
            src_ref=src, dst_ref=dst, send_sem=sends, recv_sem=recvs,
            device_id={axis: device}, device_id_type=MESH,
        )

    ring, pairs, sums, shares = {}, {}, {}, {}

    def chip_of(stage):
        return lax.rem(chip + chips - stage, chips)

    def collect(stage):
        slot = chip_of(stage) * CORES + core
        source = rhs_ref if stage == 0 else all_ref.at[slot]
        if stage > 0:
            ring[stage - 1].wait_recv()
        if stage < chips - 1:
            ring[stage] = remote(
                source, all_ref.at[slot], rsend_sem.at[stage], rrecv_sem.at[stage], "prow", right
            )
            ring[stage].start()
        pairs[stage] = remote(
            source, all_ref.at[slot], psend_sem.at[stage], precv_sem.at[stage], "prow", partner
        )
        pairs[stage].start()
        if stage == 0:
            all_ref[slot] = rhs_ref[...]
        pairs[stage].wait_recv()

    def multiply(stage):
        first = chip_of(stage) * CORES

        @pl.loop(0, width // tile)
        def _(step):
            cols = span(step, tile)
            lhs = all_ref[pl.ds(first, CORES)].reshape(rows, depth)
            value = lax.dot_general(lhs, inv_ref[cols, :], NT, preferred_element_type=F32)
            for owner in range(size):
                piece = value[owner * part : (owner + 1) * part]
                prod_ref[owner, :, cols] = piece
                send_ref[stage, owner, :, cols] = piece.astype(BF16)

        own_ref[stage] = prod_ref[place]
        for index, peer in enumerate(peers):
            sums[stage, index] = remote(
                send_ref.at[stage, peer], recv_ref.at[stage, index],
                send_sem.at[stage, index], recv_sem.at[stage, index], "pcol", peer,
            )
            sums[stage, index].start()

    def settle(stage):
        total = own_ref[stage]
        for index in range(size - 1):
            sums[stage, index].wait_recv()
            total = total + recv_ref[stage, index].astype(F32)
        full_ref[stage, place] = total.astype(BF16)
        for index, peer in enumerate(peers):
            shares[stage, index] = remote(
                full_ref.at[stage, place], full_ref.at[stage, place],
                gsend_sem.at[stage, index], grecv_sem.at[stage, index], "pcol", peer,
            )
            shares[stage, index].start()

    def couple(stage):
        for index in range(size - 1):
            shares[stage, index].wait_recv()
        target = span(chip_of(stage), rows)
        solved_ref[target, :] = full_ref[stage].reshape(rows, width)

        @pl.loop(0, count // wide)
        def _(step):
            cols = span(step, wide)
            upd_ref[target, cols] = lax.dot_general(
                solved_ref[target, :], coup_ref[:, cols], NN, preferred_element_type=F32
            ).astype(BF16)

    for stage in range(chips + 2):
        if stage < chips:
            collect(stage)
            multiply(stage)
        if 1 <= stage <= chips:
            settle(stage - 1)
        if stage >= 2:
            couple(stage - 2)
    for group in (ring, pairs, sums, shares):
        for copy in group.values():
            copy.wait_send()


def lower_kernel(
    size, line, rhs_ref, inv_ref, upper_ref, picked_ref, code_ref, out_ref,
    own_ref, send_ref, recv_ref, pass_ref, take_ref, all_ref,
    rsend_sem, rrecv_sem, psend_sem, precv_sem, send_sem, recv_sem, xsend_sem, xrecv_sem,
):
    meet((("pcol", size), ("prow", line)))
    place = lax.axis_index("prow")
    own, width = own_ref.shape
    part = own // PARTS
    share = picked_ref.shape[2]
    count = out_ref.shape[1]
    tile = tile_of(count)
    chips = line // CORES
    chip = place // CORES
    core = lax.rem(place, CORES)
    right = lax.rem(chip + 1, chips) * CORES + core
    partner = chip * CORES + (CORES - 1 - core)
    ring, pairs = [], []
    for stage in range(chips):
        slot = lax.rem(chip + chips - stage, chips) * CORES + core
        source = rhs_ref if stage == 0 else all_ref.at[slot]
        if stage > 0:
            ring[stage - 1].wait_recv()
        if stage < chips - 1:
            ring.append(
                pltpu.make_async_remote_copy(
                    src_ref=source, dst_ref=all_ref.at[slot],
                    send_sem=rsend_sem.at[stage], recv_sem=rrecv_sem.at[stage],
                    device_id={"prow": right}, device_id_type=MESH,
                )
            )
            ring[stage].start()
        pairs.append(
            pltpu.make_async_remote_copy(
                src_ref=source, dst_ref=all_ref.at[slot],
                send_sem=psend_sem.at[stage], recv_sem=precv_sem.at[stage],
                device_id={"prow": partner}, device_id_type=MESH,
            )
        )
        pairs[stage].start()
        if stage == 0:
            all_ref[slot] = rhs_ref[...]
    for copy in pairs:
        copy.wait_recv()
    copies = start_sums(
        all_ref, inv_ref, own_ref, send_ref, recv_ref, send_sem, recv_sem, size
    )
    row_ids = lax.broadcasted_iota(jnp.int32, (width, share), 0)
    moves = []
    for piece in range(PARTS):
        rows = pl.ds(piece * part, part)
        lower = finish_sum(copies, piece, own_ref, recv_ref, size)
        upper = upper_ref[rows, :]
        for step in list(range(1, line)) + [0]:
            target = lax.rem(place + step, line)
            wanted = picked_ref[target]
            low = jnp.where(row_ids == wanted, 1.0, 0.0).astype(BF16)
            high = jnp.where(row_ids + width == wanted, 1.0, 0.0).astype(BF16)
            chosen = (
                lax.dot_general(lower, low, NN, preferred_element_type=F32)
                + lax.dot_general(upper, high, NN, preferred_element_type=F32)
            ).astype(BF16)
            if step == 0:
                take_ref[0, rows, :] = chosen
                continue
            pass_ref[step - 1, rows, :] = chosen
            move = pltpu.make_async_remote_copy(
                src_ref=pass_ref.at[step - 1, rows],
                dst_ref=take_ref.at[step, rows],
                send_sem=xsend_sem.at[piece, step - 1],
                recv_sem=xrecv_sem.at[piece, step - 1],
                device_id={"prow": target},
                device_id_type=MESH,
            )
            move.start()
            moves.append(move)
    for move in moves:
        move.wait_recv()
    slot_ids = lax.broadcasted_iota(jnp.int32, (share, tile), 0)

    @pl.loop(0, count // tile)
    def _(step):
        cols = span(step, tile)
        code = code_ref[:, cols]
        total = jnp.zeros((own, tile), F32)
        for source in range(line):
            spot = jnp.where(slot_ids + source * share == code, 1.0, 0.0).astype(BF16)
            total = total + lax.dot_general(
                take_ref[source], spot, NN, preferred_element_type=F32
            )
        out_ref[:, cols] = total.astype(BF16)

    for copy in ring + pairs + list(copies.values()) + moves:
        copy.wait_send()


def params(number):
    return pltpu.CompilerParams(
        collective_id=number, has_side_effects=True, vmem_limit_bytes=60 * 1024 * 1024
    )


def in_vmem(count):
    return [pl.BlockSpec(memory_space=pltpu.VMEM)] * count


def sum_scratch(size, own, width):
    return [
        pltpu.VMEM((own, width), F32),
        pltpu.VMEM((size - 1, own, width), BF16),
        pltpu.VMEM((size - 1, own, width), BF16),
    ]


def dma(*shape):
    return pltpu.SemaphoreType.DMA(shape)


def body(right_side, inverse_blocks, coupling, pivots):
    rhs_here = right_side.shape[0]
    tile_width = right_side.shape[3]
    blocks_here = inverse_blocks.shape[1]
    count_rows = blocks_here * tile_width
    tiles_half = inverse_blocks.shape[4]
    count_cols = tiles_half * tile_width
    inverse_pair = inverse_blocks.reshape(2, count_rows, count_cols)
    coupling_mat = coupling.reshape(count_rows, count_cols)
    line = lax.axis_size("prow")
    size = lax.axis_size("pcol")
    rhs_total = rhs_here * line
    own = rhs_total // size
    me = lax.axis_index("prow")

    lower_rhs = right_side[:, :tiles_half].reshape(rhs_here, count_cols)
    upper_rhs = right_side[:, tiles_half:].astype(BF16).reshape(rhs_here, count_cols)

    own_pivots = pivots.reshape(-1)
    width = own_pivots.shape[0]
    share = width // line
    all_pivots = lax.all_gather(own_pivots, "prow", axis=0)

    def owner_of(rows):
        return rows // tile_width % line

    def local_of(rows):
        return rows // (tile_width * line) * tile_width + rows % tile_width

    mine = owner_of(all_pivots) == me
    slot = jnp.where(mine, jnp.cumsum(mine.astype(jnp.int32), axis=1) - 1, -1)
    hits = slot[:, :, None] == lax.broadcasted_iota(jnp.int32, (1, 1, share), 2)
    picked = jnp.sum(jnp.where(hits, local_of(all_pivots)[:, :, None], 0), axis=1)
    owner = owner_of(own_pivots)
    same = owner[None, :] == lax.broadcasted_iota(jnp.int32, (line, 1), 0)
    rank = jnp.sum(jnp.where(same, jnp.cumsum(same.astype(jnp.int32), axis=1) - 1, 0), axis=0)
    code = (me - owner + line) % line * share + rank

    chips = line // CORES
    part = CORES * rhs_here // size
    update_partial, upper_all = pl.pallas_call(
        functools.partial(upper_kernel, size, line),
        out_shape=(
            jax.ShapeDtypeStruct((rhs_total, count_cols), BF16),
            jax.ShapeDtypeStruct((rhs_total, count_rows), BF16),
        ),
        in_specs=in_vmem(3),
        out_specs=tuple(in_vmem(2)),
        scratch_shapes=[
            pltpu.VMEM((line, rhs_here, count_cols), BF16),
            pltpu.VMEM((size, part, count_rows), F32),
            pltpu.VMEM((chips, part, count_rows), F32),
            pltpu.VMEM((chips, size, part, count_rows), BF16),
            pltpu.VMEM((chips, size - 1, part, count_rows), BF16),
            pltpu.VMEM((chips, size, part, count_rows), BF16),
        ]
        + [dma(chips - 1)] * 2
        + [dma(chips)] * 2
        + [dma(chips, size - 1)] * 4,
        compiler_params=params(0),
        name="upper",
    )(upper_rhs, inverse_pair[1], coupling_mat)
    upper_solved = lax.dynamic_slice_in_dim(upper_all, lax.axis_index("pcol") * own, own, 0)
    update = lax.psum_scatter(update_partial, "prow", scatter_dimension=0, tiled=True)
    lower_ready = (lower_rhs - update.astype(F32)).astype(BF16)
    later_pair, _ = lax.optimization_barrier((inverse_blocks, update_partial))
    later_inverse = later_pair[0].reshape(count_rows, count_cols)
    permuted = pl.pallas_call(
        functools.partial(lower_kernel, size, line),
        out_shape=jax.ShapeDtypeStruct((own, width), BF16),
        in_specs=in_vmem(5),
        out_specs=in_vmem(1)[0],
        scratch_shapes=sum_scratch(size, own, count_rows)
        + [
            pltpu.VMEM((line - 1, own, share), BF16),
            pltpu.VMEM((line, own, share), BF16),
            pltpu.VMEM((line, rhs_here, count_cols), BF16),
        ]
        + [dma(chips - 1)] * 2
        + [dma(chips)] * 2
        + [dma(PARTS, size - 1)] * 2
        + [dma(PARTS, line - 1)] * 2,
        compiler_params=params(1),
        name="lower",
    )(lower_ready, later_inverse, upper_solved, picked.reshape(line, 1, share), code.reshape(1, width))
    return permuted.reshape(own, pivots.shape[0], 1, tile_width)


def solution(mesh):
    in_specs = (
        P("prow", None, "pcol", None),
        P(None, None, "prow", None, None, "pcol", None),
        P(None, "prow", None, None, "pcol", None),
        P(None, "prow", None),
    )
    out_specs = P("pcol", None, "prow", None)
    return jax.shard_map(body, mesh=mesh, in_specs=in_specs, out_specs=out_specs, check_vma=False)
```
